32 devices in a mesh: groups: 2 (over y), ctx: 4 (over z), dom: 2 (over x), tp: 2 (over core).
Axes of the slice: x: 2, y: 2, z: 4, core: 2. Of those that a mesh axis runs over, the one named last changes fastest.
Arguments:
- queries: bfloat16 [8, 32, 8, 8, 128], P('groups', 'dom', 'tp'), parts along dimension 0, may hold values from -8 to 8
- prompt_cache: bfloat16 [4, 8192, 8, 128], P('groups', 'ctx', 'tp'), parts along dimension 0, may hold values from -8 to 8
- suffix_cache: bfloat16 [4, 32, 16, 8, 128], P('groups', 'dom', 'ctx', 'tp'), parts along dimension 0, may hold values from -8 to 8
- new_kv: bfloat16 [8, 2, 32, 8, 128], P('groups', None, 'dom', 'tp'), parts along dimension 0, may hold values from -8 to 8
- ancestors: int32 [8, 32], P('groups'), parts along dimension 0, may hold values from 0 to 31, as said below
- lengths: int32 [64], P('groups'), parts along dimension 0, may hold values from 1 to 12, as said below
Outputs:
- attended: bfloat16 [8, 32, 8, 8, 128], P('groups', 'dom', 'tp'), parts along dimension 0
The draws below stay inside these ranges and needn't reach their ends.
There are 2 independent parts, one for each index of `groups`. The reference program is written for one: setup_inputs(seed, part) draws one part's arguments, and reference() takes and returns one part's arrays. A program takes and returns all parts, laid end to end along the dimension named above; each array names one. Nothing has to cross between parts.
Inputs may be any that keep to these rules, and one draw needn't show every extreme that they name: `ancestors`: particle p is owned by owner p // 16. In every step, of the 16 offspring of one owner at most 16 have their ancestor among the particles of any one owner, and each owner has exactly 16 from some one owner. `lengths`: the largest length is reached in every draw.
All inputs are finite; a program needn't handle non-finite values.
Results may differ from the reference program's by a relative error of at most 0.005.
Values may be sent and summed in bfloat16 or wider, within the bound.
A program may use at most 128 MiB of HBM per device.

```python
import math
import jax
import jax.numpy as jnp
from jax import lax

KVH = 8
GROUP = 8
HD = 128
PART_DEV = 16
STEPS = 4
OWNERS = 2
PARTICLES = 32
PROMPT = 8192
SUF = 16
CAP = 16


def shared_dirs(key):
    base_key = jax.random.fold_in(key, 977)
    along_key = jax.random.fold_in(base_key, 0)
    suffix_dir = (jax.random.randint(along_key, (KVH, HD), 0, 2) * 2 - 1).astype(jnp.float32)
    return suffix_dir


def suffix_shift():
    mass_ratio = max(math.log(PROMPT / SUF), 1.0)
    return math.sqrt(mass_ratio / (math.sqrt(HD) + 2.0))


def drawn_noise(noise_key, full_shape):
    return jnp.clip(jax.random.normal(noise_key, full_shape, jnp.float32), -6.0, 6.0)


def draw_queries(key, part):
    suffix_dir = shared_dirs(key)
    shift_size = suffix_shift()
    noise_key = jax.random.fold_in(jax.random.fold_in(key, 1), 0)
    full_shape = (STEPS, PARTICLES, KVH, GROUP, HD)
    direction = suffix_dir[None, None, :, None, :]
    values = 2.0 * drawn_noise(noise_key, full_shape) + shift_size * direction
    return jnp.clip(values, -8.0, 8.0).astype(jnp.bfloat16)


def draw_prompt_cache(key, part):
    noise_key = jax.random.fold_in(jax.random.fold_in(key, 2), 0)
    full_shape = (2, PROMPT, KVH, HD)
    values = drawn_noise(noise_key, full_shape)
    return jnp.clip(values, -8.0, 8.0).astype(jnp.bfloat16)


def draw_suffix_cache(key, part):
    suffix_dir = shared_dirs(key)
    shift_size = suffix_shift()
    noise_key = jax.random.fold_in(jax.random.fold_in(key, 3), 0)
    full_shape = (2, PARTICLES, SUF, KVH, HD)
    noise_part = drawn_noise(noise_key, full_shape)
    key_rows = noise_part[0] + shift_size * suffix_dir[None, None]
    values = jnp.stack([key_rows, noise_part[1]])
    return jnp.clip(values, -8.0, 8.0).astype(jnp.bfloat16)


def draw_new_kv(key, part):
    suffix_dir = shared_dirs(key)
    shift_size = suffix_shift()
    noise_key = jax.random.fold_in(jax.random.fold_in(key, 4), 0)
    full_shape = (STEPS, 2, PARTICLES, KVH, HD)
    noise_part = drawn_noise(noise_key, full_shape)
    key_rows = noise_part[:, 0] + shift_size * suffix_dir[None, None]
    values = jnp.stack([key_rows, noise_part[:, 1]], axis=1)
    return jnp.clip(values, -8.0, 8.0).astype(jnp.bfloat16)


def draw_lengths(key, part):
    value_key, pick_key = jax.random.split(jax.random.fold_in(key, 5))
    values = jax.random.randint(value_key, (PARTICLES,), 1, SUF - STEPS + 1)
    chosen = jax.random.randint(pick_key, (), 0, PARTICLES)
    return jnp.where(jnp.arange(PARTICLES) == chosen, SUF - STEPS, values).astype(jnp.int32)


def draw_ancestors(key, part):

    def one_owner(owner_key):
        first_key, other_key, order_key, local_key = jax.random.split(owner_key, 4)
        first_source = jax.random.randint(first_key, (), 0, OWNERS)
        others = (first_source + 1 + jnp.arange((OWNERS - 1) * CAP) // CAP) % OWNERS
        others = jax.random.permutation(other_key, others)[:PART_DEV - CAP]
        sources = jnp.concatenate([jnp.full((CAP,), first_source, jnp.int32), others.astype(jnp.int32)])
        sources = jax.random.permutation(order_key, sources)
        local_index = jax.random.randint(local_key, (PART_DEV,), 0, PART_DEV)
        return (sources * PART_DEV + local_index).astype(jnp.int32)

    def one_step(step_key):
        return jax.vmap(one_owner)(jax.random.split(step_key, OWNERS)).reshape(PARTICLES)
    return jax.vmap(one_step)(jax.random.split(jax.random.fold_in(key, 6), STEPS))


def setup_inputs(seed: int = 0, part: int = 0) -> dict:
    arg_keys = jax.random.split(jax.random.key(seed), 7)
    part_splits = jax.random.split(jax.random.fold_in(arg_keys[6], part), 7)
    return {
        "queries": draw_queries(jax.random.fold_in(jax.random.fold_in(arg_keys[6], part), 71), part),
        "prompt_cache": draw_prompt_cache(jax.random.fold_in(jax.random.fold_in(arg_keys[6], part), 71), part),
        "suffix_cache": draw_suffix_cache(jax.random.fold_in(jax.random.fold_in(arg_keys[6], part), 71), part),
        "new_kv": draw_new_kv(jax.random.fold_in(jax.random.fold_in(arg_keys[6], part), 71), part),
        "ancestors": draw_ancestors(jax.random.fold_in(jax.random.fold_in(arg_keys[6], part), 71), part),
        "lengths": draw_lengths(jax.random.fold_in(jax.random.fold_in(arg_keys[6], part), 71), part),
    }


def attend(query_block, prompt_cache, suffix_rows, visible, score_scale):
    operands = (jnp.moveaxis(query_block, 1, 0), jnp.moveaxis(prompt_cache[0], 1, 0), jnp.moveaxis(prompt_cache[1], 1, 0), jnp.moveaxis(suffix_rows[0], 2, 0), jnp.moveaxis(suffix_rows[1], 2, 0))

    def one_head(pieces):
        query_head, prompt_keys, prompt_values, suffix_keys, suffix_values = pieces
        query_wide = query_head.astype(jnp.float32)
        prompt_scores = jnp.einsum('pgd,td->pgt', query_wide, prompt_keys.astype(jnp.float32)) * score_scale
        suffix_scores = jnp.einsum('pgd,psd->pgs', query_wide, suffix_keys.astype(jnp.float32)) * score_scale
        suffix_scores = jnp.where(visible[:, None, :], suffix_scores, -jnp.inf)
        peak_score = jnp.maximum(lax.optimization_barrier(jnp.max(prompt_scores, axis=-1)), lax.optimization_barrier(jnp.max(suffix_scores, axis=-1)))
        prompt_exp = jnp.exp(prompt_scores - peak_score[..., None])
        suffix_exp = jnp.exp(suffix_scores - peak_score[..., None])
        totals = lax.optimization_barrier(jnp.sum(prompt_exp, axis=-1)) + lax.optimization_barrier(jnp.sum(suffix_exp, axis=-1))
        prompt_weights = lax.optimization_barrier(prompt_exp.astype(jnp.bfloat16)).astype(jnp.float32)
        suffix_weights = lax.optimization_barrier(suffix_exp.astype(jnp.bfloat16)).astype(jnp.float32)
        numerator = jnp.einsum('pgt,td->pgd', prompt_weights, prompt_values.astype(jnp.float32))
        numerator = numerator + jnp.einsum('pgs,psd->pgd', suffix_weights, suffix_values.astype(jnp.float32))
        return (numerator / totals[..., None]).astype(jnp.bfloat16)
    per_head = lax.map(one_head, operands)
    return jnp.moveaxis(per_head, 0, 1)

def reference(queries, prompt_cache, suffix_cache, new_kv, ancestors, lengths):
    score_scale = 1.0 / math.sqrt(HD)
    suffix_rows = suffix_cache
    lengths_now = lengths
    positions = jnp.arange(SUF).astype(jnp.int32)
    results = []
    for step_index in range(STEPS):
        parents = ancestors[step_index]
        suffix_rows = jnp.take(suffix_rows, parents, axis=1)
        lengths_now = jnp.take(lengths_now, parents)
        new_slot = positions[None, :] == lengths_now[:, None]
        suffix_rows = jnp.where(new_slot[None, :, :, None, None], new_kv[step_index][:, :, None], suffix_rows)
        visible = positions[None, :] <= lengths_now[:, None]
        results.append(attend(queries[step_index], prompt_cache, suffix_rows, visible, score_scale))
        lengths_now = lengths_now + 1
    return jnp.stack(results)
```

```python
import functools
import math

import jax
import jax.numpy as jnp
from jax import lax
from jax.experimental import pallas as pl
from jax.experimental.pallas import tpu as pltpu
from jax.sharding import PartitionSpec as P

MESH = pl.DeviceIdType.MESH
SG = 2
D_LOCAL, D_MERGE, D_SPREAD = 1, 2, 4
F32, BF16 = jnp.float32, jnp.bfloat16


def log2_int(n):
    assert n & (n - 1) == 0
    return n.bit_length() - 1


def nt(a, b):
    return lax.dot_general(a, b, (((1,), (1,)), ((), ())), preferred_element_type=F32)


def nn(a, b):
    return jnp.dot(a, b, preferred_element_type=F32)


def iota(shape, dim):
    return lax.broadcasted_iota(jnp.int32, shape, dim)


def kernel(
    n_ctx, owners, suf_dev, score_mul,
    q_ref, prompt_hbm, suf_hbm, new_hbm, anc_ref, len_ref, out_ref,
    raw, kf, vf, kh, vth, s_scr,
    suf_g, new_g, sfk, sfv, nfk, nfv, mask,
    acc, stat, msg, got_l, got_r, gst_l, gst_r,
    load_sem, ex_local, ex_send, ex_recv,
    rs_send, rs_recv_l, rs_recv_r, ag_send_l, ag_send_r, ag_recv,
):
    steps, per, heads, group, hd = q_ref.shape
    particles = per * owners
    prompt = kh.shape[0]
    rows = SG * per * group
    groups_of_steps = steps // SG
    nb = heads * groups_of_steps
    lo, hi = n_ctx // 2 - 1, n_ctx // 2
    z = lax.axis_index("ctx")
    me = lax.axis_index("dom")
    n_suf = particles * suf_dev
    shares = n_ctx // steps
    chunk = per // shares
    n_new = owners * chunk
    n_ext = mask.shape[1]
    my_step = z // shares
    p0 = lax.rem(z, shares) * chunk

    loads = [
        pltpu.make_async_copy(prompt_hbm.at[i], raw.at[i], load_sem.at[i]) for i in range(2)
    ]
    for c in loads:
        c.start()

    barrier = pltpu.get_barrier_semaphore()
    for d in range(1, owners):
        pl.semaphore_signal(
            barrier, inc=1, device_id={"dom": lax.rem(me + d, owners)}, device_id_type=MESH
        )

    @pl.when(z > 0)
    def _():
        pl.semaphore_signal(barrier, inc=1, device_id={"ctx": z - 1}, device_id_type=MESH)

    @pl.when(z < n_ctx - 1)
    def _():
        pl.semaphore_signal(barrier, inc=1, device_id={"ctx": z + 1}, device_id_type=MESH)

    expected = (owners - 1) + jnp.where(z > 0, 1, 0) + jnp.where(z < n_ctx - 1, 1, 0)
    pl.semaphore_wait(barrier, expected)

    if shares == 1:
        new_src = new_hbm.at[my_step]
    else:
        new_src = new_hbm.at[
            my_step, :, pl.ds(pl.multiple_of(p0 * heads, chunk * heads), chunk * heads), :
        ]
    exchange = []
    for d in range(1, owners):
        peer = {"dom": lax.rem(me + d, owners)}
        for i, (src, dst) in enumerate(((suf_hbm, suf_g), (new_src, new_g))):
            exchange.append(
                pltpu.make_async_remote_copy(
                    src_ref=src, dst_ref=dst.at[me],
                    send_sem=ex_send.at[i, d - 1], recv_sem=ex_recv.at[i, d - 1],
                    device_id=peer, device_id_type=MESH,
                )
            )
    own = [
        pltpu.make_async_copy(suf_hbm, suf_g.at[me], ex_local.at[0]),
        pltpu.make_async_copy(new_src, new_g.at[me], ex_local.at[1]),
    ]
    for c in exchange + own:
        c.start()

    key = iota((n_ext, particles), 0)
    col = iota((n_ext, particles), 1)
    suf_particle = key >> log2_int(suf_dev)
    suf_pos = (key & (suf_dev - 1)) + z * suf_dev
    reach = (key < n_suf) & (suf_particle == col) & (suf_pos < len_ref[...])
    state = jnp.where(reach, 1.0, 0.0)
    rest = key - n_suf
    new_particle = (rest >> log2_int(chunk)) * per + (rest & (chunk - 1)) + p0
    is_new = jnp.where(
        (rest >= 0) & (rest < n_new) & (new_particle == col), 1.0, 0.0
    )
    spread = jnp.where(
        iota((particles, per * group), 0)
        == (iota((particles, per * group), 1) >> log2_int(group)) + me * per,
        1.0, 0.0,
    ).astype(BF16)
    for s in range(steps):
        parents = anc_ref[pl.ds(s, 1), :]
        move = jnp.where(iota((particles, particles), 0) == parents, 1.0, 0.0).astype(BF16)
        state = nn(state.astype(BF16), move)
        state = state + is_new * jnp.where(my_step == s, 1.0, 0.0)
        wide = nn(state.astype(BF16), spread)
        mask[s] = jnp.where(wide > 0.5, 0.0, -1e30)

    for src, dst in ((0, kf), (1, vf)):
        loads[src].wait()
        size = 1024

        def widen(i, _, src=src, dst=dst):
            at = pl.ds(pl.multiple_of(i * size, size), size)
            dst[at, :] = raw[src, at, :].astype(F32)
            return 0

        lax.fori_loop(0, raw.shape[1] // size, widen, 0)

    def parts(b):
        h = b // groups_of_steps
        return h, (b - h * groups_of_steps) * SG

    def queries_of(b):
        h, s0 = parts(b)
        out = [
            q_ref[s0 + i, :, h].astype(F32).reshape(per * group, hd) for i in range(SG)
        ]
        return jnp.concatenate(out, axis=0).astype(BF16)

    def prompt_stage(b):
        h, s0 = parts(b)

        @pl.when(s0 == 0)
        def _():
            size = 256
            for i in range(prompt // size):
                at = pl.ds(h + i * size * heads, size, stride=heads)
                kh[pl.ds(i * size, size), :] = kf[at, :].astype(BF16)
                vth[:, pl.ds(i * size, size)] = vf[at, :].T.astype(BF16)

        q = queries_of(b)
        size = 512
        top = None
        for i in range(prompt // size):
            at = pl.ds(i * size, size)
            s = nt(kh[at, :], q)
            s_scr[at, :] = s
            t = jnp.max(s, axis=0, keepdims=True)
            top = t if top is None else jnp.maximum(top, t)
        top = top * score_mul
        total = jnp.zeros((1, rows), F32)
        numer = jnp.zeros((hd, rows), F32)
        for i in range(prompt // size):
            at = pl.ds(i * size, size)
            w = jnp.exp2(s_scr[at, :] * score_mul - top)
            total += jnp.sum(w, axis=0, keepdims=True)
            numer += nn(vth[:, at], w.astype(BF16))
        acc[b] = numer
        put_stat(b, top, total)

    def put_stat(b, top, total):
        stat[b] = jnp.where(iota((8, rows), 0) == 0, top, total)

    def merge(first, second):
        m1, l1, a1 = first
        m2, l2, a2 = second
        m = jnp.maximum(m1, m2)
        c1, c2 = jnp.exp2(m1 - m), jnp.exp2(m2 - m)
        return m, l1 * c1 + l2 * c2, a1 * c1 + a2 * c2

    def held(b):
        return stat[b, 0:1, :], stat[b, 1:2, :], acc[b]

    def rs_copies(b, right):
        data, small = (got_l, gst_l) if right else (got_r, gst_r)
        sems = rs_recv_l if right else rs_recv_r
        peer = {"ctx": z + 1} if right else {"ctx": z - 1}
        return [
            pltpu.make_async_remote_copy(
                src_ref=src.at[b], dst_ref=dst.at[b],
                send_sem=rs_send.at[i, b], recv_sem=sems.at[i, b],
                device_id=peer, device_id_type=MESH,
            )
            for i, (src, dst) in enumerate(((stat, small), (msg, data)))
        ]

    def owner_of(b):
        return jnp.where(lax.rem(b, 2) == 0, lo, hi)

    def send_partial(b):
        @pl.when(z < owner_of(b))
        def _():
            for c in rs_copies(b, True):
                c.start()

        @pl.when(z > owner_of(b))
        def _():
            for c in rs_copies(b, False):
                c.start()

    def unpack_extra():
        for c in own:
            c.wait()
        for c in exchange:
            c.wait()
        ps, pn = suf_g.shape[2], new_g.shape[2]
        for o in range(owners):
            for i, dst in enumerate((sfk, sfv)):
                dst[pl.ds(o * ps, ps), :] = suf_g[o, i].astype(F32)
            for i, dst in enumerate((nfk, nfv)):
                dst[pl.ds(o * pn, pn), :] = new_g[o, i].astype(F32)

    def local_stage(b):
        @pl.when(b == 0)
        def _():
            unpack_extra()

        h, s0 = parts(b)
        pad = jnp.zeros((n_ext - n_suf - n_new, hd), F32)

        def rows_of(suf, new):
            pieces = [suf[pl.ds(h, n_suf, stride=heads), :], new[pl.ds(h, n_new, stride=heads), :]]
            return jnp.concatenate(pieces + ([pad] if pad.shape[0] else []), axis=0)

        ks = rows_of(sfk, nfk).astype(BF16)
        vt = rows_of(sfv, nfv).T.astype(BF16)
        bias = jnp.concatenate([mask[s0 + i] for i in range(SG)], axis=1)
        s = nt(ks, queries_of(b)) * score_mul + bias
        top = jnp.max(s, axis=0, keepdims=True)
        old_top, old_total, old_numer = held(b)
        new_top = jnp.maximum(old_top, top)
        w = jnp.exp2(s - new_top)
        keep = jnp.exp2(old_top - new_top)
        total = old_total * keep + jnp.sum(w, axis=0, keepdims=True)
        numer = old_numer * keep + nn(vt, w.astype(BF16))
        put_stat(b, new_top, total)
        acc[b] = numer
        msg[b] = numer.astype(BF16)

        @pl.when((z == 0) | (z == n_ctx - 1))
        def _():
            @pl.when(z != owner_of(b))
            def _():
                send_partial(b)

    def recv_partial(b, from_left):
        data, small = (got_l, gst_l) if from_left else (got_r, gst_r)
        for c in rs_copies(b, from_left):
            c.wait_recv()
        top, total, numer = merge(
            held(b), (small[b, 0:1, :], small[b, 1:2, :], data[b].astype(F32))
        )
        put_stat(b, top, total)
        acc[b] = numer

    def ag_copy(b, right, i):
        h, s0 = parts(b)
        at = out_ref.at[s0 + i, :, h]
        sems = ag_send_r if right else ag_send_l
        return pltpu.make_async_remote_copy(
            src_ref=at, dst_ref=at,
            send_sem=sems.at[i, b], recv_sem=ag_recv.at[i, b],
            device_id={"ctx": z + 1} if right else {"ctx": z - 1}, device_id_type=MESH,
        )

    def ag_send(b):
        for i in range(SG):
            @pl.when((z <= owner_of(b)) & (z > 0))
            def _():
                ag_copy(b, False, i).start()

            @pl.when((z >= owner_of(b)) & (z < n_ctx - 1))
            def _():
                ag_copy(b, True, i).start()

    def merge_stage(b):
        owner = owner_of(b)

        @pl.when((z > 0) & (z <= owner))
        def _():
            recv_partial(b, True)

        @pl.when((z < n_ctx - 1) & (z >= owner))
        def _():
            recv_partial(b, False)

        @pl.when((z != owner) & (z > 0) & (z < n_ctx - 1))
        def _():
            msg[b] = acc[b].astype(BF16)
            send_partial(b)

        @pl.when(z == owner)
        def _():
            _, total, numer = held(b)
            h, s0 = parts(b)
            done = numer / total
            for i in range(SG):
                wide = done[:, i * per * group:(i + 1) * per * group].T
                out_ref[s0 + i, :, h] = wide.reshape(per, group, hd).astype(BF16)
            ag_send(b)

    def spread_stage(b):
        owner = owner_of(b)

        @pl.when(z != owner)
        def _():
            for i in range(SG):
                ag_copy(b, True, i).wait_recv()
            ag_send(b)

    def finish(b):
        owner = owner_of(b)

        @pl.when(z != owner)
        def _():
            for c in rs_copies(b, True):
                c.wait_send()

        for i in range(SG):
            @pl.when((z <= owner) & (z > 0))
            def _():
                ag_copy(b, False, i).wait_send()

            @pl.when((z >= owner) & (z < n_ctx - 1))
            def _():
                ag_copy(b, True, i).wait_send()

    def run(i, _):
        for delay, stage in (
            (0, prompt_stage), (D_LOCAL, local_stage), (D_MERGE, merge_stage), (D_SPREAD, spread_stage)
        ):
            @pl.when((i >= delay) & (i < nb + delay))
            def _(delay=delay, stage=stage):
                stage(i - delay)
        return 0

    lax.fori_loop(0, nb + D_SPREAD, run, 0)

    def close(b, _):
        finish(b)
        return 0

    lax.fori_loop(0, nb, close, 0)


def on_device(n_ctx, owners, queries, prompt_cache, suffix_cache, new_kv, ancestors, lengths):
    steps, per, heads, group, hd = queries.shape
    prompt = prompt_cache.shape[1]
    suf_dev = suffix_cache.shape[2]
    particles = ancestors.shape[1]
    rows = SG * per * group
    nb = heads * (steps // SG)
    shares = n_ctx // steps
    chunk = per // shares
    n_ext = -(-(particles * suf_dev + owners * chunk) // 128) * 128
    dma = pltpu.SemaphoreType.DMA
    score_mul = math.log2(math.e) / math.sqrt(hd)
    ps, pn = per * suf_dev * heads, chunk * heads
    any_spec = pl.BlockSpec(memory_space=pl.ANY)
    vmem_spec = pl.BlockSpec(memory_space=pltpu.VMEM)
    return pl.pallas_call(
        functools.partial(kernel, n_ctx, owners, suf_dev, score_mul),
        out_shape=jax.ShapeDtypeStruct(queries.shape, BF16),
        in_specs=[vmem_spec, any_spec, any_spec, any_spec, vmem_spec, vmem_spec],
        out_specs=vmem_spec,
        scratch_shapes=[
            pltpu.VMEM((2, prompt * heads, hd), BF16),
            pltpu.VMEM((prompt * heads, hd), F32),
            pltpu.VMEM((prompt * heads, hd), F32),
            pltpu.VMEM((prompt, hd), BF16),
            pltpu.VMEM((hd, prompt), BF16),
            pltpu.VMEM((prompt, rows), F32),
            pltpu.VMEM((owners, 2, ps, hd), BF16),
            pltpu.VMEM((owners, 2, pn, hd), BF16),
            pltpu.VMEM((owners * ps, hd), F32),
            pltpu.VMEM((owners * ps, hd), F32),
            pltpu.VMEM((owners * pn, hd), F32),
            pltpu.VMEM((owners * pn, hd), F32),
            pltpu.VMEM((steps, n_ext, per * group), F32),
            pltpu.VMEM((nb, hd, rows), F32),
            pltpu.VMEM((nb, 8, rows), F32),
            pltpu.VMEM((nb, hd, rows), BF16),
            pltpu.VMEM((nb, hd, rows), BF16),
            pltpu.VMEM((nb, hd, rows), BF16),
            pltpu.VMEM((nb, 8, rows), F32),
            pltpu.VMEM((nb, 8, rows), F32),
            dma((2,)),
            dma((2,)),
            dma((2, max(owners - 1, 1))),
            dma((2, max(owners - 1, 1))),
            dma((2, nb)),
            dma((2, nb)),
            dma((2, nb)),
            dma((SG, nb)),
            dma((SG, nb)),
            dma((SG, nb)),
        ],
        compiler_params=pltpu.CompilerParams(
            collective_id=0, has_side_effects=True, vmem_limit_bytes=60 << 20
        ),
    )(
        queries,
        prompt_cache.reshape(2, prompt * heads, hd),
        suffix_cache.reshape(2, ps, hd),
        new_kv.reshape(steps, 2, per * heads, hd),
        ancestors,
        lengths.reshape(1, particles),
    )


def solution(mesh):
    return jax.shard_map(
        functools.partial(on_device, mesh.shape["ctx"], mesh.shape["dom"]),
        mesh=mesh,
        in_specs=(
            P("groups", "dom", "tp", None, None),
            P("groups", "ctx", "tp", None),
            P("groups", "dom", "ctx", "tp", None),
            P("groups", None, "dom", "tp", None),
            P("groups", None),
            P("groups"),
        ),
        out_specs=P("groups", "dom", "tp", None, None),
        check_vma=False,
    )
```

```python
import functools
import math

import jax
import jax.numpy as jnp
from jax import lax
from jax.experimental import pallas as pl
from jax.experimental.pallas import tpu as pltpu
from jax.sharding import PartitionSpec as P

MESH = pl.DeviceIdType.MESH
SG = 2
CS = 1
AHEAD = 4
D_FOLD, D_SWAP = 5, 7
F32, BF16 = jnp.float32, jnp.bfloat16


def log2_int(n):
    assert n & (n - 1) == 0
    return n.bit_length() - 1


def nt(a, b):
    return lax.dot_general(a, b, (((1,), (1,)), ((), ())), preferred_element_type=F32)


def nn(a, b):
    return jnp.dot(a, b, preferred_element_type=F32)


def iota(shape, dim):
    return lax.broadcasted_iota(jnp.int32, shape, dim)


def kernel(
    n_ctx, owners, suf_dev, score_mul,
    q_ref, prompt_hbm, suf_hbm, new_hbm, anc_ref, len_ref, out_ref,
    raw, kf, vf, kh, vth, kx, vx, s_scr,
    suf_g, new_g, sfk, sfv, nfk, nfv, mask,
    acc, stat, msg, got_out, got_in, gst_out, gst_in, fin,
    load_sem, ex_local, ex_send, ex_recv,
    rs_send, rs_recv_out, rs_recv_in, ag_send, ag_recv,
):
    steps, per, heads, group, hd = q_ref.shape
    particles = per * owners
    prompt = kh.shape[0]
    rows = SG * per * group
    groups_of_steps = steps // SG
    nb = heads * groups_of_steps
    cuts = SG // CS
    width = CS * per * group
    lo, hi = n_ctx // 2 - 1, n_ctx // 2
    z = lax.axis_index("ctx")
    me = lax.axis_index("dom")
    n_suf = particles * suf_dev
    shares = n_ctx // steps
    chunk = per // shares
    n_new = owners * chunk
    n_ext = mask.shape[1]
    my_step = z // shares
    p0 = lax.rem(z, shares) * chunk

    loads = [
        pltpu.make_async_copy(prompt_hbm.at[i], raw.at[i], load_sem.at[i]) for i in range(2)
    ]
    for c in loads:
        c.start()

    barrier = pltpu.get_barrier_semaphore()
    for d in range(1, owners):
        pl.semaphore_signal(
            barrier, inc=1, device_id={"dom": lax.rem(me + d, owners)}, device_id_type=MESH
        )

    @pl.when(z > 0)
    def _():
        pl.semaphore_signal(barrier, inc=1, device_id={"ctx": z - 1}, device_id_type=MESH)

    @pl.when(z < n_ctx - 1)
    def _():
        pl.semaphore_signal(barrier, inc=1, device_id={"ctx": z + 1}, device_id_type=MESH)

    expected = (owners - 1) + jnp.where(z > 0, 1, 0) + jnp.where(z < n_ctx - 1, 1, 0)
    pl.semaphore_wait(barrier, expected)

    if shares == 1:
        new_src = new_hbm.at[my_step]
    else:
        new_src = new_hbm.at[
            my_step, :, pl.ds(pl.multiple_of(p0 * heads, chunk * heads), chunk * heads), :
        ]
    exchange = []
    for d in range(1, owners):
        peer = {"dom": lax.rem(me + d, owners)}
        for i, (src, dst) in enumerate(((suf_hbm, suf_g), (new_src, new_g))):
            exchange.append(
                pltpu.make_async_remote_copy(
                    src_ref=src, dst_ref=dst.at[me],
                    send_sem=ex_send.at[i, d - 1], recv_sem=ex_recv.at[i, d - 1],
                    device_id=peer, device_id_type=MESH,
                )
            )
    own = [
        pltpu.make_async_copy(suf_hbm, suf_g.at[me], ex_local.at[0]),
        pltpu.make_async_copy(new_src, new_g.at[me], ex_local.at[1]),
    ]
    for c in exchange + own:
        c.start()

    key = iota((n_ext, particles), 0)
    col = iota((n_ext, particles), 1)
    suf_particle = key >> log2_int(suf_dev)
    suf_pos = (key & (suf_dev - 1)) + z * suf_dev
    reach = (key < n_suf) & (suf_particle == col) & (suf_pos < len_ref[...])
    state = jnp.where(reach, 1.0, 0.0)
    rest = key - n_suf
    new_particle = (rest >> log2_int(chunk)) * per + (rest & (chunk - 1)) + p0
    is_new = jnp.where(
        (rest >= 0) & (rest < n_new) & (new_particle == col), 1.0, 0.0
    )
    spread = jnp.where(
        iota((particles, per * group), 0)
        == (iota((particles, per * group), 1) >> log2_int(group)) + me * per,
        1.0, 0.0,
    ).astype(BF16)
    for s in range(steps):
        parents = anc_ref[pl.ds(s, 1), :]
        move = jnp.where(iota((particles, particles), 0) == parents, 1.0, 0.0).astype(BF16)
        state = nn(state.astype(BF16), move)
        state = state + is_new * jnp.where(my_step == s, 1.0, 0.0)
        wide = nn(state.astype(BF16), spread)
        mask[s] = jnp.where(wide > 0.5, 0.0, -1e30)

    for src, dst in ((0, kf), (1, vf)):
        loads[src].wait()
        size = 1024

        def widen(i, _, src=src, dst=dst):
            at = pl.ds(pl.multiple_of(i * size, size), size)
            dst[at, :] = raw[src, at, :].astype(F32)
            return 0

        lax.fori_loop(0, raw.shape[1] // size, widen, 0)

    def parts(b):
        h = b // groups_of_steps
        return h, (b - h * groups_of_steps) * SG

    def queries_of(b):
        h, s0 = parts(b)
        out = [
            q_ref[s0 + i, :, h].astype(F32).reshape(per * group, hd) for i in range(SG)
        ]
        return jnp.concatenate(out, axis=0).astype(BF16)

    def extra_rows(suf, new, h):
        pieces = [suf[pl.ds(h, n_suf, stride=heads), :], new[pl.ds(h, n_new, stride=heads), :]]
        if n_ext > n_suf + n_new:
            pieces.append(jnp.zeros((n_ext - n_suf - n_new, hd), F32))
        return jnp.concatenate(pieces, axis=0)

    def bias_of(s0):
        return jnp.concatenate([mask[s0 + i] for i in range(SG)], axis=1)

    def prompt_stage(b, extra):
        h, s0 = parts(b)

        @pl.when(s0 == 0)
        def _():
            size = 256
            for i in range(prompt // size):
                at = pl.ds(h + i * size * heads, size, stride=heads)
                kh[pl.ds(i * size, size), :] = kf[at, :].astype(BF16)
                vth[:, pl.ds(i * size, size)] = vf[at, :].T.astype(BF16)
            if extra:
                kx[...] = extra_rows(sfk, nfk, h).astype(BF16)
                vx[...] = extra_rows(sfv, nfv, h).T.astype(BF16)

        q = queries_of(b)
        size = 512
        top = None
        if extra:
            sx = nt(kx[...], q) * score_mul + bias_of(s0)
        for i in range(prompt // size):
            at = pl.ds(i * size, size)
            s = nt(kh[at, :], q)
            s_scr[at, :] = s
            t = jnp.max(s, axis=0, keepdims=True)
            top = t if top is None else jnp.maximum(top, t)
        top = top * score_mul
        total = jnp.zeros((1, rows), F32)
        numer = jnp.zeros((hd, rows), F32)
        if extra:
            top = jnp.maximum(top, jnp.max(sx, axis=0, keepdims=True))
            w = jnp.exp2(sx - top)
            total += jnp.sum(w, axis=0, keepdims=True)
            numer += nn(vx[...], w.astype(BF16))
        for i in range(prompt // size):
            at = pl.ds(i * size, size)
            w = jnp.exp2(s_scr[at, :] * score_mul - top)
            total += jnp.sum(w, axis=0, keepdims=True)
            numer += nn(vth[:, at], w.astype(BF16))
        put(b, top, total, numer, extra)
        if extra:
            start_inward(b)

    def put(b, top, total, numer, ready):
        small = jnp.where(iota((8, rows), 0) == 0, top, total)
        for i in range(cuts):
            at = slice(i * width, (i + 1) * width)
            stat[b * cuts + i] = small[:, at]
            acc[b * cuts + i] = numer[:, at]
            if ready:
                msg[b * cuts + i] = numer[:, at].astype(BF16)

    def unpack_extra():
        for c in own:
            c.wait()
        for c in exchange:
            c.wait()
        ps, pn = suf_g.shape[2], new_g.shape[2]
        for o in range(owners):
            for i, dst in enumerate((sfk, sfv)):
                dst[pl.ds(o * ps, ps), :] = suf_g[o, i].astype(F32)
            for i, dst in enumerate((nfk, nfv)):
                dst[pl.ds(o * pn, pn), :] = new_g[o, i].astype(F32)

    def local_stage(b):
        h, s0 = parts(b)
        ks = extra_rows(sfk, nfk, h).astype(BF16)
        vt = extra_rows(sfv, nfv, h).T.astype(BF16)
        s = nt(ks, queries_of(b)) * score_mul + bias_of(s0)
        small = jnp.concatenate([stat[b * cuts + i] for i in range(cuts)], axis=1)
        old_numer = jnp.concatenate([acc[b * cuts + i] for i in range(cuts)], axis=1)
        old_top, old_total = small[0:1], small[1:2]
        new_top = jnp.maximum(old_top, jnp.max(s, axis=0, keepdims=True))
        w = jnp.exp2(s - new_top)
        keep = jnp.exp2(old_top - new_top)
        total = old_total * keep + jnp.sum(w, axis=0, keepdims=True)
        numer = old_numer * keep + nn(vt, w.astype(BF16))
        put(b, new_top, total, numer, True)
        start_inward(b)

    mid = (z == lo) | (z == hi)
    left_half = z <= lo
    inner = jnp.where(left_half, z + 1, z - 1)
    outer = jnp.where(left_half, z - 1, z + 1)
    has_outer = (z > 0) & (z < n_ctx - 1)

    def inward(c, across):
        data, small, sems = (
            (got_in, gst_in, rs_recv_in) if across else (got_out, gst_out, rs_recv_out)
        )
        return [
            pltpu.make_async_remote_copy(
                src_ref=src.at[c], dst_ref=dst.at[c],
                send_sem=rs_send.at[i, c], recv_sem=sems.at[i, c],
                device_id={"ctx": inner}, device_id_type=MESH,
            )
            for i, (src, dst) in enumerate(((stat, small), (msg, data)))
        ]

    def outward(c):
        return pltpu.make_async_remote_copy(
            src_ref=fin.at[c], dst_ref=fin.at[c],
            send_sem=ag_send.at[c], recv_sem=ag_recv.at[c],
            device_id={"ctx": outer}, device_id_type=MESH,
        )

    def start_inward(b):
        @pl.when(jnp.logical_not(has_outer))
        def _():
            for i in range(cuts):
                send(b * cuts + i)

    def send(c):
        for across in (True, False):
            @pl.when(mid if across else jnp.logical_not(mid))
            def _(across=across):
                for copy in inward(c, across):
                    copy.start()

    def merge(first, second):
        m1, l1, a1 = first
        m2, l2, a2 = second
        m = jnp.maximum(m1, m2)
        c1, c2 = jnp.exp2(m1 - m), jnp.exp2(m2 - m)
        return m, l1 * c1 + l2 * c2, a1 * c1 + a2 * c2

    def fold_stage(c):
        @pl.when(has_outer)
        def _():
            for copy in inward(c, False):
                copy.wait_recv()
            top, total, numer = merge(
                (stat[c, 0:1, :], stat[c, 1:2, :], acc[c]),
                (gst_out[c, 0:1, :], gst_out[c, 1:2, :], got_out[c].astype(F32)),
            )
            stat[c] = jnp.where(iota((8, width), 0) == 0, top, total)
            msg[c] = numer.astype(BF16)
            send(c)

    def put_out(c):
        h = c // (groups_of_steps * cuts)
        s0 = (c - h * (groups_of_steps * cuts)) * CS
        for i in range(CS):
            out_ref[s0 + i, :, h] = fin[c, i]

    def swap_stage(c):
        @pl.when(mid)
        def _():
            for copy in inward(c, True):
                copy.wait_recv()
            mine = (stat[c], msg[c].astype(F32))
            theirs = (gst_in[c], got_in[c].astype(F32))
            low = [jnp.where(left_half, a, b) for a, b in zip(mine, theirs)]
            high = [jnp.where(left_half, b, a) for a, b in zip(mine, theirs)]
            _, total, numer = merge(
                (low[0][0:1], low[0][1:2], low[1]), (high[0][0:1], high[0][1:2], high[1])
            )
            done = numer / total
            for i in range(CS):
                wide = done[:, i * per * group:(i + 1) * per * group].T
                fin[c, i] = wide.reshape(per, group, hd).astype(BF16)

            @pl.when(has_outer)
            def _():
                outward(c).start()

            put_out(c)

    def spread_stage(c):
        @pl.when(jnp.logical_not(mid))
        def _():
            outward(c).wait_recv()

            @pl.when(has_outer)
            def _():
                outward(c).start()

            put_out(c)

        for across in (True, False):
            @pl.when(mid if across else jnp.logical_not(mid))
            def _(across=across):
                for copy in inward(c, across):
                    copy.wait_send()

        @pl.when(has_outer)
        def _():
            outward(c).wait_send()

    def each(stage, b):
        for i in range(cuts):
            stage(b * cuts + i)

    def run(i, _):
        @pl.when(i < AHEAD)
        def _():
            prompt_stage(i, False)

        @pl.when(i == AHEAD)
        def _():
            unpack_extra()

            def add(b, _):
                local_stage(b)
                return 0

            lax.fori_loop(0, AHEAD, add, 0)

        @pl.when((i >= AHEAD) & (i < nb))
        def _():
            prompt_stage(i, True)

        for delay, stage in ((D_FOLD, fold_stage), (D_SWAP, swap_stage)):
            @pl.when((i >= delay) & (i < nb + delay))
            def _(delay=delay, stage=stage):
                each(stage, i - delay)
        return 0

    lax.fori_loop(0, nb + D_SWAP, run, 0)

    def close(c, _):
        spread_stage(c)
        return 0

    lax.fori_loop(0, nb * cuts, close, 0)


def on_device(n_ctx, owners, queries, prompt_cache, suffix_cache, new_kv, ancestors, lengths):
    steps, per, heads, group, hd = queries.shape
    prompt = prompt_cache.shape[1]
    suf_dev = suffix_cache.shape[2]
    particles = ancestors.shape[1]
    rows = SG * per * group
    nc = heads * (steps // CS)
    width = CS * per * group
    shares = n_ctx // steps
    chunk = per // shares
    n_ext = -(-(particles * suf_dev + owners * chunk) // 128) * 128
    dma = pltpu.SemaphoreType.DMA
    score_mul = math.log2(math.e) / math.sqrt(hd)
    ps, pn = per * suf_dev * heads, chunk * heads
    any_spec = pl.BlockSpec(memory_space=pl.ANY)
    vmem_spec = pl.BlockSpec(memory_space=pltpu.VMEM)
    return pl.pallas_call(
        functools.partial(kernel, n_ctx, owners, suf_dev, score_mul),
        out_shape=jax.ShapeDtypeStruct(queries.shape, BF16),
        in_specs=[vmem_spec, any_spec, any_spec, any_spec, vmem_spec, vmem_spec],
        out_specs=vmem_spec,
        scratch_shapes=[
            pltpu.VMEM((2, prompt * heads, hd), BF16),
            pltpu.VMEM((prompt * heads, hd), F32),
            pltpu.VMEM((prompt * heads, hd), F32),
            pltpu.VMEM((prompt, hd), BF16),
            pltpu.VMEM((hd, prompt), BF16),
            pltpu.VMEM((n_ext, hd), BF16),
            pltpu.VMEM((hd, n_ext), BF16),
            pltpu.VMEM((prompt, rows), F32),
            pltpu.VMEM((owners, 2, ps, hd), BF16),
            pltpu.VMEM((owners, 2, pn, hd), BF16),
            pltpu.VMEM((owners * ps, hd), F32),
            pltpu.VMEM((owners * ps, hd), F32),
            pltpu.VMEM((owners * pn, hd), F32),
            pltpu.VMEM((owners * pn, hd), F32),
            pltpu.VMEM((steps, n_ext, per * group), F32),
            pltpu.VMEM((nc, hd, width), F32),
            pltpu.VMEM((nc, 8, width), F32),
            pltpu.VMEM((nc, hd, width), BF16),
            pltpu.VMEM((nc, hd, width), BF16),
            pltpu.VMEM((nc, hd, width), BF16),
            pltpu.VMEM((nc, 8, width), F32),
            pltpu.VMEM((nc, 8, width), F32),
            pltpu.VMEM((nc, CS, per, group, hd), BF16),
            dma((2,)),
            dma((2,)),
            dma((2, max(owners - 1, 1))),
            dma((2, max(owners - 1, 1))),
            dma((2, nc)),
            dma((2, nc)),
            dma((2, nc)),
            dma((nc,)),
            dma((nc,)),
        ],
        compiler_params=pltpu.CompilerParams(
            collective_id=0, has_side_effects=True, vmem_limit_bytes=60 << 20
        ),
    )(
        queries,
        prompt_cache.reshape(2, prompt * heads, hd),
        suffix_cache.reshape(2, ps, hd),
        new_kv.reshape(steps, 2, per * heads, hd),
        ancestors,
        lengths.reshape(1, particles),
    )


def solution(mesh):
    return jax.shard_map(
        functools.partial(on_device, mesh.shape["ctx"], mesh.shape["dom"]),
        mesh=mesh,
        in_specs=(
            P("groups", "dom", "tp", None, None),
            P("groups", "ctx", "tp", None),
            P("groups", "dom", "ctx", "tp", None),
            P("groups", None, "dom", "tp", None),
            P("groups", None),
            P("groups"),
        ),
        out_specs=P("groups", "dom", "tp", None, None),
        check_vma=False,
    )
```

```python
import functools
import math

import jax
import jax.numpy as jnp
from jax import lax
from jax.experimental import pallas as pl
from jax.experimental.pallas import tpu as pltpu
from jax.sharding import PartitionSpec as P

MESH = pl.DeviceIdType.MESH
SG = 2
CS = 2
AHEAD = 2
D_FOLD, D_SWAP = 2, 5
F32, BF16 = jnp.float32, jnp.bfloat16


def log2_int(n):
    assert n & (n - 1) == 0
    return n.bit_length() - 1


def nt(a, b):
    return lax.dot_general(a, b, (((1,), (1,)), ((), ())), preferred_element_type=F32)


def nn(a, b):
    return jnp.dot(a, b, preferred_element_type=F32)


def iota(shape, dim):
    return lax.broadcasted_iota(jnp.int32, shape, dim)


def kernel(
    n_ctx, owners, suf_dev, score_mul,
    q_ref, prompt_hbm, suf_hbm, new_hbm, anc_ref, len_ref, out_ref,
    raw, kf, vf, kh, vth, kx, vx, s_scr,
    suf_g, new_g, sfk, sfv, nfk, nfv, mask,
    acc, stat, msg, got_out, got_in, gst_out, gst_in, fin,
    load_sem, ex_local, ex_send, ex_recv,
    rs_send, rs_recv_out, rs_recv_in, ag_send, ag_recv,
):
    steps, per, heads, group, hd = q_ref.shape
    particles = per * owners
    prompt = kh.shape[0]
    rows = SG * per * group
    groups_of_steps = steps // SG
    nb = heads * groups_of_steps
    cuts = SG // CS
    width = CS * per * group
    lo, hi = n_ctx // 2 - 1, n_ctx // 2
    z = lax.axis_index("ctx")
    me = lax.axis_index("dom")
    n_suf = particles * suf_dev
    shares = n_ctx // steps
    chunk = per // shares
    n_new = owners * chunk
    n_ext = mask.shape[1]
    my_step = z // shares
    p0 = lax.rem(z, shares) * chunk

    loads = [
        pltpu.make_async_copy(prompt_hbm.at[i], raw.at[i], load_sem.at[i]) for i in range(2)
    ]
    for c in loads:
        c.start()

    barrier = pltpu.get_barrier_semaphore()
    for d in range(1, owners):
        pl.semaphore_signal(
            barrier, inc=1, device_id={"dom": lax.rem(me + d, owners)}, device_id_type=MESH
        )

    @pl.when(z > 0)
    def _():
        pl.semaphore_signal(barrier, inc=1, device_id={"ctx": z - 1}, device_id_type=MESH)

    @pl.when(z < n_ctx - 1)
    def _():
        pl.semaphore_signal(barrier, inc=1, device_id={"ctx": z + 1}, device_id_type=MESH)

    expected = (owners - 1) + jnp.where(z > 0, 1, 0) + jnp.where(z < n_ctx - 1, 1, 0)
    pl.semaphore_wait(barrier, expected)

    if shares == 1:
        new_src = new_hbm.at[my_step]
    else:
        new_src = new_hbm.at[
            my_step, :, pl.ds(pl.multiple_of(p0 * heads, chunk * heads), chunk * heads), :
        ]
    exchange = []
    for d in range(1, owners):
        peer = {"dom": lax.rem(me + d, owners)}
        for i, (src, dst) in enumerate(((suf_hbm, suf_g), (new_src, new_g))):
            exchange.append(
                pltpu.make_async_remote_copy(
                    src_ref=src, dst_ref=dst.at[me],
                    send_sem=ex_send.at[i, d - 1], recv_sem=ex_recv.at[i, d - 1],
                    device_id=peer, device_id_type=MESH,
                )
            )
    own = [
        pltpu.make_async_copy(suf_hbm, suf_g.at[me], ex_local.at[0]),
        pltpu.make_async_copy(new_src, new_g.at[me], ex_local.at[1]),
    ]
    for c in exchange + own:
        c.start()

    key = iota((n_ext, particles), 0)
    col = iota((n_ext, particles), 1)
    suf_particle = key >> log2_int(suf_dev)
    suf_pos = (key & (suf_dev - 1)) + z * suf_dev
    reach = (key < n_suf) & (suf_particle == col) & (suf_pos < len_ref[...])
    state = jnp.where(reach, 1.0, 0.0)
    rest = key - n_suf
    new_particle = (rest >> log2_int(chunk)) * per + (rest & (chunk - 1)) + p0
    is_new = jnp.where(
        (rest >= 0) & (rest < n_new) & (new_particle == col), 1.0, 0.0
    )
    spread = jnp.where(
        iota((particles, per * group), 0)
        == (iota((particles, per * group), 1) >> log2_int(group)) + me * per,
        1.0, 0.0,
    ).astype(BF16)
    for s in range(steps):
        parents = anc_ref[pl.ds(s, 1), :]
        move = jnp.where(iota((particles, particles), 0) == parents, 1.0, 0.0).astype(BF16)
        state = nn(state.astype(BF16), move)
        state = state + is_new * jnp.where(my_step == s, 1.0, 0.0)
        wide = nn(state.astype(BF16), spread)
        mask[s] = jnp.where(wide > 0.5, 0.0, -1e30)

    for src, dst in ((0, kf), (1, vf)):
        loads[src].wait()
        size = 1024

        def widen(i, _, src=src, dst=dst):
            at = pl.ds(pl.multiple_of(i * size, size), size)
            dst[at, :] = raw[src, at, :].astype(F32)
            return 0

        lax.fori_loop(0, raw.shape[1] // size, widen, 0)

    def parts(b):
        h = b // groups_of_steps
        return h, (b - h * groups_of_steps) * SG

    def queries_of(b):
        h, s0 = parts(b)
        out = [
            q_ref[s0 + i, :, h].astype(F32).reshape(per * group, hd) for i in range(SG)
        ]
        return jnp.concatenate(out, axis=0).astype(BF16)

    def extra_rows(suf, new, h):
        pieces = [suf[pl.ds(h, n_suf, stride=heads), :], new[pl.ds(h, n_new, stride=heads), :]]
        if n_ext > n_suf + n_new:
            pieces.append(jnp.zeros((n_ext - n_suf - n_new, hd), F32))
        return jnp.concatenate(pieces, axis=0)

    def bias_of(s0):
        return jnp.concatenate([mask[s0 + i] for i in range(SG)], axis=1)

    def prompt_stage(b, extra):
        h, s0 = parts(b)

        @pl.when(s0 == 0)
        def _():
            size = 256
            for i in range(prompt // size):
                at = pl.ds(h + i * size * heads, size, stride=heads)
                kh[pl.ds(i * size, size), :] = kf[at, :].astype(BF16)
                vth[:, pl.ds(i * size, size)] = vf[at, :].T.astype(BF16)
            if extra:
                kx[...] = extra_rows(sfk, nfk, h).astype(BF16)
                vx[...] = extra_rows(sfv, nfv, h).T.astype(BF16)

        q = queries_of(b)
        size = 512
        top = None
        if extra:
            sx = nt(kx[...], q) * score_mul + bias_of(s0)
        for i in range(prompt // size):
            at = pl.ds(i * size, size)
            s = nt(kh[at, :], q)
            s_scr[at, :] = s
            t = jnp.max(s, axis=0, keepdims=True)
            top = t if top is None else jnp.maximum(top, t)
        top = top * score_mul
        total = jnp.zeros((1, rows), F32)
        numer = jnp.zeros((hd, rows), F32)
        if extra:
            top = jnp.maximum(top, jnp.max(sx, axis=0, keepdims=True))
            w = jnp.exp2(sx - top)
            total += jnp.sum(w, axis=0, keepdims=True)
            numer += nn(vx[...], w.astype(BF16))
        for i in range(prompt // size):
            at = pl.ds(i * size, size)
            w = jnp.exp2(s_scr[at, :] * score_mul - top)
            total += jnp.sum(w, axis=0, keepdims=True)
            numer += nn(vth[:, at], w.astype(BF16))
        put(b, top, total, numer, extra)
        if extra:
            start_inward(b)

    def put(b, top, total, numer, ready):
        small = jnp.where(iota((2, rows), 0) == 0, top, total)
        for i in range(cuts):
            at = slice(i * width, (i + 1) * width)
            stat[b * cuts + i] = small[:, at]
            acc[b * cuts + i] = numer[:, at]
            if ready:
                msg[b * cuts + i] = numer[:, at].astype(BF16)

    def unpack_extra():
        for c in own:
            c.wait()
        for c in exchange:
            c.wait()
        ps, pn = suf_g.shape[2], new_g.shape[2]
        for o in range(owners):
            for i, dst in enumerate((sfk, sfv)):
                dst[pl.ds(o * ps, ps), :] = suf_g[o, i].astype(F32)
            for i, dst in enumerate((nfk, nfv)):
                dst[pl.ds(o * pn, pn), :] = new_g[o, i].astype(F32)

    def local_stage(b):
        h, s0 = parts(b)
        ks = extra_rows(sfk, nfk, h).astype(BF16)
        vt = extra_rows(sfv, nfv, h).T.astype(BF16)
        s = nt(ks, queries_of(b)) * score_mul + bias_of(s0)
        small = jnp.concatenate([stat[b * cuts + i] for i in range(cuts)], axis=1)
        old_numer = jnp.concatenate([acc[b * cuts + i] for i in range(cuts)], axis=1)
        old_top, old_total = small[0:1], small[1:2]
        new_top = jnp.maximum(old_top, jnp.max(s, axis=0, keepdims=True))
        w = jnp.exp2(s - new_top)
        keep = jnp.exp2(old_top - new_top)
        total = old_total * keep + jnp.sum(w, axis=0, keepdims=True)
        numer = old_numer * keep + nn(vt, w.astype(BF16))
        put(b, new_top, total, numer, True)
        start_inward(b)

    mid = (z == lo) | (z == hi)
    left_half = z <= lo
    inner = jnp.where(left_half, z + 1, z - 1)
    outer = jnp.where(left_half, z - 1, z + 1)
    has_outer = (z > 0) & (z < n_ctx - 1)

    def inward(c, across):
        data, small, sems = (
            (got_in, gst_in, rs_recv_in) if across else (got_out, gst_out, rs_recv_out)
        )
        return [
            pltpu.make_async_remote_copy(
                src_ref=src.at[c], dst_ref=dst.at[c],
                send_sem=rs_send.at[i, c], recv_sem=sems.at[i, c],
                device_id={"ctx": inner}, device_id_type=MESH,
            )
            for i, (src, dst) in enumerate(((stat, small), (msg, data)))
        ]

    def outward(c):
        return pltpu.make_async_remote_copy(
            src_ref=fin.at[c], dst_ref=fin.at[c],
            send_sem=ag_send.at[c], recv_sem=ag_recv.at[c],
            device_id={"ctx": outer}, device_id_type=MESH,
        )

    def start_inward(b):
        @pl.when(jnp.logical_not(has_outer))
        def _():
            for i in range(cuts):
                send(b * cuts + i)

    def send(c):
        for across in (True, False):
            @pl.when(mid if across else jnp.logical_not(mid))
            def _(across=across):
                for copy in inward(c, across):
                    copy.start()

    def merge(first, second):
        m1, l1, a1 = first
        m2, l2, a2 = second
        m = jnp.maximum(m1, m2)
        c1, c2 = jnp.exp2(m1 - m), jnp.exp2(m2 - m)
        return m, l1 * c1 + l2 * c2, a1 * c1 + a2 * c2

    def fold_stage(c):
        @pl.when(has_outer)
        def _():
            for copy in inward(c, False):
                copy.wait_recv()
            top, total, numer = merge(
                (stat[c, 0:1, :], stat[c, 1:2, :], acc[c]),
                (gst_out[c, 0:1, :], gst_out[c, 1:2, :], got_out[c].astype(F32)),
            )
            stat[c] = jnp.where(iota((2, width), 0) == 0, top, total)
            msg[c] = numer.astype(BF16)
            send(c)

    def put_out(c):
        h = c // (groups_of_steps * cuts)
        s0 = (c - h * (groups_of_steps * cuts)) * CS
        for i in range(CS):
            out_ref[s0 + i, :, h] = fin[c, i]

    def swap_stage(c):
        @pl.when(mid)
        def _():
            for copy in inward(c, True):
                copy.wait_recv()
            mine = (stat[c], msg[c].astype(F32))
            theirs = (gst_in[c], got_in[c].astype(F32))
            low = [jnp.where(left_half, a, b) for a, b in zip(mine, theirs)]
            high = [jnp.where(left_half, b, a) for a, b in zip(mine, theirs)]
            _, total, numer = merge(
                (low[0][0:1], low[0][1:2], low[1]), (high[0][0:1], high[0][1:2], high[1])
            )
            done = numer / total
            for i in range(CS):
                wide = done[:, i * per * group:(i + 1) * per * group].T
                fin[c, i] = wide.reshape(per, group, hd).astype(BF16)

            @pl.when(has_outer)
            def _():
                outward(c).start()

            put_out(c)

    def spread_stage(c):
        @pl.when(jnp.logical_not(mid))
        def _():
            outward(c).wait_recv()

            @pl.when(has_outer)
            def _():
                outward(c).start()

            put_out(c)

        for across in (True, False):
            @pl.when(mid if across else jnp.logical_not(mid))
            def _(across=across):
                for copy in inward(c, across):
                    copy.wait_send()

        @pl.when(has_outer)
        def _():
            outward(c).wait_send()

    def each(stage, b):
        for i in range(cuts):
            stage(b * cuts + i)

    def run(i, _):
        @pl.when(i < AHEAD)
        def _():
            prompt_stage(i, False)

        @pl.when(i == AHEAD)
        def _():
            unpack_extra()

            def add(b, _):
                local_stage(b)
                return 0

            lax.fori_loop(0, AHEAD, add, 0)

        @pl.when((i >= AHEAD) & (i < nb))
        def _():
            prompt_stage(i, True)

        for delay, stage in ((D_FOLD, fold_stage), (D_SWAP, swap_stage)):
            @pl.when((i >= delay) & (i < nb + delay))
            def _(delay=delay, stage=stage):
                each(stage, i - delay)
        return 0

    lax.fori_loop(0, nb + D_SWAP, run, 0)

    def close(c, _):
        spread_stage(c)
        return 0

    lax.fori_loop(0, nb * cuts, close, 0)


def on_device(n_ctx, owners, queries, prompt_cache, suffix_cache, new_kv, ancestors, lengths):
    steps, per, heads, group, hd = queries.shape
    prompt = prompt_cache.shape[1]
    suf_dev = suffix_cache.shape[2]
    particles = ancestors.shape[1]
    rows = SG * per * group
    nc = heads * (steps // CS)
    width = CS * per * group
    shares = n_ctx // steps
    chunk = per // shares
    n_ext = -(-(particles * suf_dev + owners * chunk) // 128) * 128
    dma = pltpu.SemaphoreType.DMA
    score_mul = math.log2(math.e) / math.sqrt(hd)
    ps, pn = per * suf_dev * heads, chunk * heads
    any_spec = pl.BlockSpec(memory_space=pl.ANY)
    vmem_spec = pl.BlockSpec(memory_space=pltpu.VMEM)
    return pl.pallas_call(
        functools.partial(kernel, n_ctx, owners, suf_dev, score_mul),
        out_shape=jax.ShapeDtypeStruct(queries.shape, BF16),
        in_specs=[vmem_spec, any_spec, any_spec, any_spec, vmem_spec, vmem_spec],
        out_specs=vmem_spec,
        scratch_shapes=[
            pltpu.VMEM((2, prompt * heads, hd), BF16),
            pltpu.VMEM((prompt * heads, hd), F32),
            pltpu.VMEM((prompt * heads, hd), F32),
            pltpu.VMEM((prompt, hd), BF16),
            pltpu.VMEM((hd, prompt), BF16),
            pltpu.VMEM((n_ext, hd), BF16),
            pltpu.VMEM((hd, n_ext), BF16),
            pltpu.VMEM((prompt, rows), F32),
            pltpu.VMEM((owners, 2, ps, hd), BF16),
            pltpu.VMEM((owners, 2, pn, hd), BF16),
            pltpu.VMEM((owners * ps, hd), F32),
            pltpu.VMEM((owners * ps, hd), F32),
            pltpu.VMEM((owners * pn, hd), F32),
            pltpu.VMEM((owners * pn, hd), F32),
            pltpu.VMEM((steps, n_ext, per * group), F32),
            pltpu.VMEM((nc, hd, width), F32),
            pltpu.VMEM((nc, 2, width), F32),
            pltpu.VMEM((nc, hd, width), BF16),
            pltpu.VMEM((nc, hd, width), BF16),
            pltpu.VMEM((nc, hd, width), BF16),
            pltpu.VMEM((nc, 2, width), F32),
            pltpu.VMEM((nc, 2, width), F32),
            pltpu.VMEM((nc, CS, per, group, hd), BF16),
            dma((2,)),
            dma((2,)),
            dma((2, max(owners - 1, 1))),
            dma((2, max(owners - 1, 1))),
            dma((2, nc)),
            dma((2, nc)),
            dma((2, nc)),
            dma((nc,)),
            dma((nc,)),
        ],
        compiler_params=pltpu.CompilerParams(
            collective_id=0, has_side_effects=True, vmem_limit_bytes=60 << 20
        ),
    )(
        queries,
        prompt_cache.reshape(2, prompt * heads, hd),
        suffix_cache.reshape(2, ps, hd),
        new_kv.reshape(steps, 2, per * heads, hd),
        ancestors,
        lengths.reshape(1, particles),
    )


def solution(mesh):
    return jax.shard_map(
        functools.partial(on_device, mesh.shape["ctx"], mesh.shape["dom"]),
        mesh=mesh,
        in_specs=(
            P("groups", "dom", "tp", None, None),
            P("groups", "ctx", "tp", None),
            P("groups", "dom", "ctx", "tp", None),
            P("groups", None, "dom", "tp", None),
            P("groups", None),
            P("groups"),
        ),
        out_specs=P("groups", "dom", "tp", None, None),
        check_vma=False,
    )
```
